32 devices in a mesh: row: 4 (over z), col: 8 (over y, x, core).
Axes of the slice: x: 2, y: 2, z: 4, core: 2. Of those that a mesh axis runs over, the one named last changes fastest.
Arguments:
- tokens: bfloat16 [512, 8192], P('col', 'row'), may hold values from -6 to 6
- modality: int32 [512], P('row'), may hold values 0 or 1
- in_weight: bfloat16 [8192, 2, 28672], P('row', None, 'col'), may hold values from -0.0625 to 0.0625
- down_weight: bfloat16 [28672, 8192], P('col', 'row'), may hold values from -0.03125 to 0.03125
- d_mixed: bfloat16 [512, 8192], P('col', 'row'), may hold values from -6 to 6
Outputs:
- mixed: bfloat16 [512, 8192], P('col', 'row')
- d_down: bfloat16 [28672, 8192], P('col', 'row')
- d_in: bfloat16 [8192, 2, 28672], P('row', None, 'col')
- d_tokens: bfloat16 [512, 8192], P('col', 'row')
The draws below stay inside these ranges and needn't reach their ends.
All inputs are finite; a program needn't handle non-finite values. No bound on the sum of `modality` on one device may be relied on, other than what follows from the above.
Results may differ from the reference program's by a relative error of at most 0.0049.
Values may be sent and summed in bfloat16 or wider, within the bound.
A program may use at most 192 MiB of HBM per device.

```python
import jax
import jax.numpy as jnp

D = 8192
FF = 28672
TOKENS = 512


def touch_ends(result, rng, least, top_value):
    index_at = [jax.random.randint(jax.random.fold_in(rng, axis), (), 0, length) for axis, length in enumerate(result.shape)]
    longest = result.shape.index(max(result.shape))
    next_to = index_at[:longest] + [(index_at[longest] + 1) % result.shape[longest]] + index_at[longest + 1:]
    return result.at[tuple(index_at)].set(least).at[tuple(next_to)].set(top_value)


def block_levels(key, shape, cuts, low, high):
    factor_of, own = 1.0, jax.random.fold_in(key, 6)
    for position, shards_of in cuts:
        steps = jnp.exp(jax.random.uniform(jax.random.fold_in(own, position), (shards_of,), jnp.float32, low / len(cuts), high / len(cuts)))
        factor_of = factor_of * jnp.repeat(steps, shape[position] // shards_of).reshape([-1 if axis == position else 1 for axis in range(len(shape))])
    return factor_of


def noise(key, shape, scale, bound, split=(), held_as=jnp.bfloat16):
    drawn = scale * jax.random.normal(key, shape, jnp.float32)
    if split:
        drawn = drawn * block_levels(key, shape, split, -0.22, 0.18)
    return jnp.clip(drawn, -bound, bound).astype(held_as)


def setup_inputs(seed: int = 0) -> dict:
    key_of = jax.random.split(jax.random.key(seed), 6)
    tokens = noise(key_of[0], (TOKENS, D), 1.0, 6.0, ((0, 8), (1, 4)))
    modality = touch_ends((jax.random.randint(key_of[1], (TOKENS,), 0, 2) < 1).astype(jnp.int32), jax.random.fold_in(key_of[1], 1), 0, 1)
    in_weight = noise(key_of[2], (D, 2, FF), D ** -0.5, 0.0625, ((0, 4), (2, 8)))
    down_weight = noise(key_of[3], (FF, D), FF ** -0.5, 0.03125, ((0, 8), (1, 4)))
    d_mixed = noise(key_of[4], (TOKENS, D), 1.0, 6.0, ((0, 8), (1, 4)))
    return {"tokens": tokens, "modality": modality, "in_weight": in_weight, "down_weight": down_weight, "d_mixed": d_mixed}


def reference(tokens, modality, in_weight, down_weight, d_mixed):
    selected = (modality == 1).astype(jnp.float32)[:, None]
    flat_in = in_weight.reshape(D, 2 * FF)
    projected = jnp.dot(tokens, flat_in, preferred_element_type=jnp.float32)
    gate_part = projected[:, :FF]
    up_part = projected[:, FF:]
    sigmoid_gate = jax.nn.sigmoid(gate_part)
    activated = gate_part * sigmoid_gate
    hidden = (selected * activated * up_part).astype(jnp.bfloat16)
    mixed = jnp.dot(hidden, down_weight, preferred_element_type=jnp.float32).astype(jnp.bfloat16)
    d_down = jnp.dot(hidden.T, d_mixed, preferred_element_type=jnp.float32).astype(jnp.bfloat16)
    d_hidden = jnp.dot(d_mixed, down_weight.T, preferred_element_type=jnp.float32)
    d_scaled = selected * d_hidden
    d_gate = d_scaled * up_part * (sigmoid_gate + gate_part * sigmoid_gate * (1.0 - sigmoid_gate))
    d_up = d_scaled * activated
    d_projected = jnp.concatenate([d_gate, d_up], 1).astype(jnp.bfloat16)
    d_in = jnp.dot(tokens.T, d_projected, preferred_element_type=jnp.float32).reshape(D, 2, FF).astype(jnp.bfloat16)
    d_tokens = jnp.dot(d_projected, flat_in.T, preferred_element_type=jnp.float32).astype(jnp.bfloat16)
    return mixed, d_down, d_in, d_tokens
```

```python
import jax
import jax.numpy as jnp
from jax import lax
from jax.sharding import PartitionSpec as P


def exchange(partial, axis):
    count = lax.axis_size(axis)
    me = lax.axis_index(axis)
    rows = partial.shape[0] // count
    received = []
    for shift in range(1, count):
        start = lax.rem(me + shift, count) * rows
        block = lax.dynamic_slice_in_dim(partial, start, rows, 0).astype(jnp.bfloat16)
        moves = [(i, (i + shift) % count) for i in range(count)]
        received.append(lax.ppermute(block, axis, moves))
    total = lax.dynamic_slice_in_dim(partial, me * rows, rows, 0)
    for block in received:
        total = total + block.astype(jnp.float32)
    return total


def block_terms(rows, cotangents, in_weight, down_weight, spread):
    width = in_weight.shape[2]
    flat_in = in_weight.reshape(in_weight.shape[0], 2 * width)
    d_hidden = exchange(
        jnp.einsum("td,fd->tf", cotangents, down_weight, preferred_element_type=jnp.float32), "row"
    )
    projected = exchange(jnp.dot(rows, flat_in, preferred_element_type=jnp.float32), "row")
    gate_part = projected[:, :width]
    up_part = projected[:, width:]
    sigmoid_gate = jax.nn.sigmoid(gate_part)
    activated = gate_part * sigmoid_gate
    hidden = (activated * up_part).astype(jnp.bfloat16)
    d_gate = d_hidden * up_part * (sigmoid_gate + gate_part * sigmoid_gate * (1.0 - sigmoid_gate))
    d_local = jnp.concatenate([d_gate, d_hidden * activated], 1).astype(jnp.bfloat16)
    hidden_all = lax.all_gather(hidden, "row", axis=0, tiled=True)
    d_projected = lax.all_gather(d_local, "row", axis=0, tiled=True)
    mixed = lax.psum_scatter(
        jnp.dot(spread(hidden_all), down_weight, preferred_element_type=jnp.float32),
        "col",
        scatter_dimension=0,
        tiled=True,
    ).astype(jnp.bfloat16)
    d_down = jnp.einsum(
        "tf,td->fd", hidden_all, cotangents, preferred_element_type=jnp.float32
    ).astype(jnp.bfloat16)
    d_tokens = lax.psum_scatter(
        jnp.einsum("tk,dk->td", spread(d_projected), flat_in, preferred_element_type=jnp.float32),
        "col",
        scatter_dimension=0,
        tiled=True,
    ).astype(jnp.bfloat16)
    d_in = jnp.einsum("td,tk->dk", rows, d_projected, preferred_element_type=jnp.float32)
    d_in = lax.optimization_barrier(d_in.astype(jnp.bfloat16))
    return (mixed, d_down, d_in.reshape(in_weight.shape), d_tokens)


def per_device(tokens, modality, in_weight, down_weight, d_mixed):
    cotangent_all = lax.all_gather(d_mixed, "col", axis=0, tiled=True)
    rows_all = lax.all_gather(tokens, "col", axis=0, tiled=True)
    chosen = lax.all_gather(modality, "row", axis=0, tiled=True) == 1
    total = chosen.shape[0]
    place = jnp.cumsum(chosen.astype(jnp.int32)) - 1
    packed = total * 5 // 8

    def packed_form(rows, cotangents, w_in, w_down):
        pick = (chosen[None, :] & (place[None, :] == jnp.arange(packed)[:, None])).astype(jnp.bfloat16)
        take = lambda x: jnp.dot(pick, x, preferred_element_type=jnp.float32).astype(jnp.bfloat16)
        spread = lambda x: jnp.einsum(
            "ct,cf->tf", pick, x, preferred_element_type=jnp.float32
        ).astype(jnp.bfloat16)
        return block_terms(take(rows), take(cotangents), w_in, w_down, spread)

    def whole_form(rows, cotangents, w_in, w_down):
        keep = chosen[:, None].astype(jnp.bfloat16)
        return block_terms(rows * keep, cotangents * keep, w_in, w_down, lambda x: x)

    return lax.cond(
        place[-1] < packed, packed_form, whole_form, rows_all, cotangent_all, in_weight, down_weight
    )


def solution(mesh):
    return jax.shard_map(
        per_device,
        mesh=mesh,
        in_specs=(
            P("col", "row"),
            P("row"),
            P("row", None, "col"),
            P("col", "row"),
            P("col", "row"),
        ),
        out_specs=(P("col", "row"), P("col", "row"), P("row", None, "col"), P("col", "row")),
        check_vma=False,
    )
```

```python
import jax
import jax.numpy as jnp
from jax import lax
from jax.experimental import pallas as pl
from jax.sharding import PartitionSpec as P


def exchange(partial, axis):
    count = lax.axis_size(axis)
    me = lax.axis_index(axis)
    rows = partial.shape[0] // count
    received = []
    for shift in range(1, count):
        start = lax.rem(me + shift, count) * rows
        block = lax.dynamic_slice_in_dim(partial, start, rows, 0).astype(jnp.bfloat16)
        moves = [(i, (i + shift) % count) for i in range(count)]
        received.append(lax.ppermute(block, axis, moves))
    total = lax.dynamic_slice_in_dim(partial, me * rows, rows, 0)
    for block in received:
        total = total + block.astype(jnp.float32)
    return total


def paired_columns(rows_ref, gate_ref, up_ref, out_ref):
    over_rows = (((0,), (0,)), ((), ()))
    for part, side_ref in enumerate((gate_ref, up_ref)):
        out_ref[:, part, :] = lax.dot_general(
            rows_ref[...], side_ref[...], over_rows, preferred_element_type=jnp.float32
        ).astype(jnp.bfloat16)


def in_gradient(rows, d_projected):
    count, depth = rows.shape
    width = d_projected.shape[1] // 2
    deep = depth // 8
    wide = max(w for w in range(128, 2049, 128) if width % w == 0)
    return pl.pallas_call(
        paired_columns,
        grid=(width // wide, depth // deep),
        in_specs=[
            pl.BlockSpec((count, deep), lambda j, i: (0, i)),
            pl.BlockSpec((count, wide), lambda j, i: (0, j)),
            pl.BlockSpec((count, wide), lambda j, i: (0, j + width // wide)),
        ],
        out_specs=pl.BlockSpec((deep, 2, wide), lambda j, i: (i, 0, j)),
        out_shape=jax.ShapeDtypeStruct((depth, 2, width), jnp.bfloat16),
        cost_estimate=pl.CostEstimate(
            flops=4 * count * depth * width,
            bytes_accessed=4 * (depth * width + count * width + count * depth),
            transcendentals=0,
        ),
    )(rows, d_projected, d_projected)


def block_terms(rows, cotangents, flat_in, down_weight, spread):
    width = flat_in.shape[1] // 2
    d_hidden = jnp.einsum("td,fd->tf", cotangents, down_weight, preferred_element_type=jnp.float32)
    d_hidden = exchange(d_hidden, "row")
    projected = exchange(jnp.dot(rows, flat_in, preferred_element_type=jnp.float32), "row")
    gate_part = projected[:, :width]
    up_part = projected[:, width:]
    sigmoid_gate = jax.nn.sigmoid(gate_part)
    activated = gate_part * sigmoid_gate
    hidden = (activated * up_part).astype(jnp.bfloat16)
    d_gate = d_hidden * up_part * (sigmoid_gate + gate_part * sigmoid_gate * (1.0 - sigmoid_gate))
    d_local = jnp.concatenate([d_gate, d_hidden * activated], 1).astype(jnp.bfloat16)
    hidden_all = lax.all_gather(hidden, "row", axis=0, tiled=True)
    d_projected = lax.all_gather(d_local, "row", axis=0, tiled=True)
    mixed = exchange(
        jnp.dot(spread(hidden_all), down_weight, preferred_element_type=jnp.float32), "col"
    ).astype(jnp.bfloat16)
    d_down = jnp.einsum(
        "tf,td->fd", hidden_all, cotangents, preferred_element_type=jnp.float32
    ).astype(jnp.bfloat16)
    d_down, d_projected = lax.optimization_barrier((d_down, d_projected))
    d_tokens = exchange(
        jnp.einsum("tk,dk->td", spread(d_projected), flat_in, preferred_element_type=jnp.float32), "col"
    ).astype(jnp.bfloat16)
    return (mixed, d_down, in_gradient(rows, d_projected), d_tokens)


def per_device(tokens, modality, in_weight, down_weight, d_mixed):
    every = lambda x: lax.all_gather(x, "col", axis=0, tiled=True)
    rows_all = every(tokens)
    chosen = lax.all_gather(modality, "row", axis=0, tiled=True) == 1
    total = chosen.shape[0]
    flat_in = lax.optimization_barrier(in_weight.reshape(in_weight.shape[0], -1))
    every = lambda x: lax.all_gather(x, "col", axis=0, tiled=True)
    place = jnp.cumsum(chosen.astype(jnp.int32)) - 1
    packed = total * 5 // 8

    def packed_form(rows, cotangents, w_in, w_down):
        pick = (chosen[None, :] & (place[None, :] == jnp.arange(packed)[:, None])).astype(jnp.bfloat16)
        take = lambda x: jnp.dot(pick, x, preferred_element_type=jnp.float32).astype(jnp.bfloat16)
        spread = lambda x: jnp.einsum(
            "ct,cf->tf", pick, x, preferred_element_type=jnp.float32
        ).astype(jnp.bfloat16)
        return block_terms(take(rows), take(every(cotangents)), w_in, w_down, spread)

    def whole_form(rows, cotangents, w_in, w_down):
        keep = chosen[:, None].astype(jnp.bfloat16)
        return block_terms(rows * keep, every(cotangents) * keep, w_in, w_down, lambda x: x)

    return lax.cond(
        place[-1] < packed, packed_form, whole_form, rows_all, d_mixed, flat_in, down_weight
    )


def solution(mesh):
    return jax.shard_map(
        per_device,
        mesh=mesh,
        in_specs=(
            P("col", "row"),
            P("row"),
            P("row", None, "col"),
            P("col", "row"),
            P("col", "row"),
        ),
        out_specs=(P("col", "row"), P("col", "row"), P("row", None, "col"), P("col", "row")),
        check_vma=False,
    )
```
